128 devices in a mesh: pa: 16 (over x_lo, y, core), row: 8 (over z, x_hi).
Axes of the slice: x: 4 (x_hi: 2, x_lo: 2; x = x_hi * 2 + x_lo), y: 4, z: 4, core: 2. Of those that a mesh axis runs over, the one named last changes fastest.
Arguments:
- echoes: bfloat16 [2, 4096, 256, 128], P(None, 'row', 'pa'), may hold values from -6 to 6
- chirp_phase: float32 [256], replicated, may hold values from -3.140625 to 3.140625
Outputs:
- covariance: float32 [256, 2, 128, 128], P(('pa', 'row'))
The draws below stay inside these ranges and needn't reach their ends.
All inputs are finite; a program needn't handle non-finite values.
Results may differ from the reference program's by a relative error of at most 0.0016.
Values may be sent and summed in bfloat16 or wider, within the bound.
No kernel may reach another device: no remote copies, remote signals or barrier semaphores. Data moves between devices by JAX's collectives and lax.ppermute only.
A program may use at most 64 MiB of HBM per device.

```python
import math
import jax
import jax.numpy as jnp
from jax import lax

E = 128
PULSES = 256
TAPS = 256
TOTAL_GATES = 4096


def steps_of(own_key, shape, split, smallest, largest):
    level, own = 1.0, jax.random.fold_in(own_key, 6)
    for dim, shards_of in split:
        steps = jnp.exp(jax.random.uniform(jax.random.fold_in(own, dim), (shards_of,), jnp.float32, smallest / len(split), largest / len(split)))
        level = level * jnp.repeat(steps, shape[dim] // shards_of).reshape([-1 if axis == dim else 1 for axis in range(len(shape))])
    return level


def bell_draw(rng, shape, spread, reach, split=(), kind=jnp.bfloat16):
    level = steps_of(rng, shape, split, -0.22, 0.18) if split else 1.0
    drawn = jax.random.normal(rng, shape, jnp.float32) * spread * level
    return jnp.minimum(jnp.maximum(drawn, -reach), reach).astype(kind)


def setup_inputs(seed: int = 0) -> dict:
    splits = jax.random.split(jax.random.key(seed), 3)
    return {
        "echoes": bell_draw(splits[0], (2, TOTAL_GATES, PULSES, E), 1.0, 6.0, ((1, 8), (2, 16))),
        "chirp_phase": jnp.clip(jax.random.uniform(splits[1], (TAPS,), jnp.float32, -3.140625, 3.140625), -3.140625, 3.140625),
    }


def filter_parts(chirp_phase):
    scaling = 1.0 / math.sqrt(chirp_phase.shape[0])
    real_part = (jnp.cos(chirp_phase) * scaling).astype(jnp.bfloat16)
    imag_part = (-jnp.sin(chirp_phase) * scaling).astype(jnp.bfloat16)
    return (real_part, imag_part)

def banded_filter(real_part, imag_part, out_rows):
    tap_count = real_part.shape[0]
    in_rows = out_rows + tap_count - 1

    def banded(values):
        padded = jnp.concatenate([values, jnp.zeros((in_rows + 1 - tap_count,), values.dtype)])
        repeated = jnp.tile(padded, out_rows)[:out_rows * in_rows]
        return repeated.reshape(out_rows, in_rows)
    real_band = banded(real_part)
    imag_band = banded(imag_part)
    upper_half = jnp.concatenate([real_band, -imag_band], axis=1)
    lower_half = jnp.concatenate([imag_band, real_band], axis=1)
    return jnp.concatenate([upper_half, lower_half], axis=0)

def doppler_matrix(pulses):
    indices = jnp.arange(pulses, dtype=jnp.int32)
    products = indices[:, None] * indices[None, :] % pulses
    angles = 2.0 * math.pi / pulses * products.astype(jnp.float32)
    scaling = 1.0 / math.sqrt(pulses)
    real_part = (jnp.cos(angles) * scaling).astype(jnp.bfloat16)
    imag_part = (-jnp.sin(angles) * scaling).astype(jnp.bfloat16)
    upper_half = jnp.stack([real_part, -imag_part], axis=1)
    lower_half = jnp.stack([imag_part, real_part], axis=1)
    return jnp.stack([upper_half, lower_half], axis=0)

def hermitian_parts(blocks_product):
    real_sum = blocks_product[:, 0, :, 0, :] + blocks_product[:, 1, :, 1, :]
    imag_sum = blocks_product[:, 1, :, 0, :] - blocks_product[:, 0, :, 1, :]
    return jnp.stack([real_sum, imag_sum], axis=1)

def reference(echoes, chirp_phase):
    total_gates = echoes.shape[1]
    pulses = echoes.shape[2]
    element_count = echoes.shape[3]
    tap_count = chirp_phase.shape[0]
    tile_rows = math.gcd(128, total_gates)
    real_part, imag_part = filter_parts(chirp_phase)
    banded = banded_filter(real_part, imag_part, tile_rows).astype(jnp.float32)
    padded = jnp.concatenate([echoes, jnp.zeros((2, tap_count - 1, pulses, element_count), echoes.dtype)], axis=1)
    matrix = doppler_matrix(pulses).astype(jnp.float32)

    def one_tile(offset):
        window = lax.dynamic_slice_in_dim(padded, offset, tile_rows + tap_count - 1, 1).astype(jnp.float32)
        flattened = window.reshape(2 * (tile_rows + tap_count - 1), pulses * element_count)
        compressed = jnp.dot(banded, flattened, preferred_element_type=jnp.float32, precision=lax.Precision.HIGHEST)
        compressed = lax.optimization_barrier(compressed.astype(jnp.bfloat16))
        compressed = compressed.astype(jnp.float32).reshape(2, tile_rows, pulses, element_count)
        spectrum = jnp.einsum('xbyp,ygpe->xgbe', matrix, compressed, precision=lax.Precision.HIGHEST)
        return spectrum.astype(jnp.bfloat16)
    starts = jnp.arange(total_gates // tile_rows, dtype=jnp.int32) * tile_rows
    spectra = lax.map(one_tile, starts)
    bin_group = 8

    def bin_block(offset):
        bin_slice = lax.dynamic_slice_in_dim(spectra, offset, bin_group, 3).astype(jnp.float32)
        blocks_product = jnp.einsum('nxgbi,nygbj->bxiyj', bin_slice, bin_slice, precision=lax.Precision.HIGHEST)
        return hermitian_parts(blocks_product) / total_gates
    bin_starts = jnp.arange(pulses // bin_group, dtype=jnp.int32) * bin_group
    grouped = lax.map(bin_block, bin_starts)
    return grouped.reshape(pulses, 2, element_count, element_count)
```

```python
import functools
import math

import jax
import jax.numpy as jnp
import numpy as np
from jax import lax
from jax.experimental import pallas as pl
from jax.experimental.pallas import tpu as pltpu
from jax.sharding import PartitionSpec as P


def filter_parts(chirp_phase):
    scaling = 1.0 / math.sqrt(chirp_phase.shape[0])
    real_part = (jnp.cos(chirp_phase) * scaling).astype(jnp.bfloat16)
    imag_part = (-jnp.sin(chirp_phase) * scaling).astype(jnp.bfloat16)
    return (real_part, imag_part)


def doppler_matrix(pulses):
    indices = np.arange(pulses)
    products = indices[:, None] * indices[None, :] % pulses
    angles = (np.float32(2.0 * math.pi / pulses) * products.astype(np.float32)).astype(np.float64)
    scaling = 1.0 / math.sqrt(pulses)
    real_part = (np.cos(angles) * scaling).astype(np.float32)
    imag_part = (-np.sin(angles) * scaling).astype(np.float32)
    upper_half = np.stack([real_part, -imag_part], axis=1)
    lower_half = np.stack([imag_part, real_part], axis=1)
    matrix = np.stack([upper_half, lower_half], axis=1)
    return matrix.reshape(2 * pulses, 2 * pulses).astype(jnp.bfloat16)


def doppler_kernel(matrix_ref, samples_ref, out_ref, scratch):
    rows = matrix_ref.shape[0]
    gates, element_count = out_ref.shape[1:]
    matrix = matrix_ref[...]

    def columns(gate):
        parts = [samples_ref[:, part, gate].reshape(-1, element_count) for part in range(2)]
        return jnp.concatenate(parts, axis=0)

    for gate in range(0, gates, 2):
        both = jnp.concatenate([columns(gate), columns(gate + 1)], axis=1)
        product = jnp.dot(matrix, both, preferred_element_type=jnp.float32)
        for k in range(2):
            scratch[gate + k] = product[:, k * element_count : (k + 1) * element_count]
    step = 32
    for row in range(0, rows, step):
        block = scratch[:, row : row + step, :]
        out_ref[row : row + step] = jnp.transpose(block, (1, 0, 2)).astype(jnp.bfloat16)


def doppler(matrix, samples):
    owners, _, gates, pulses_dev, element_count = samples.shape
    rows = matrix.shape[0]
    block = math.gcd(16, gates)
    return pl.pallas_call(
        doppler_kernel,
        out_shape=jax.ShapeDtypeStruct((rows, gates, element_count), jnp.bfloat16),
        grid=(gates // block,),
        in_specs=[
            pl.BlockSpec(matrix.shape, lambda i: (0, 0)),
            pl.BlockSpec(
                (owners, 2, block, pulses_dev, element_count), lambda i: (0, 0, i, 0, 0)
            ),
        ],
        out_specs=pl.BlockSpec((rows, block, element_count), lambda i: (0, i, 0)),
        scratch_shapes=[pltpu.VMEM((block, rows, element_count), jnp.float32)],
        compiler_params=pltpu.CompilerParams(vmem_limit_bytes=48 << 20),
        name="doppler",
    )(matrix, samples)


def covariance_kernel(total_gates, taps_ref, samples_ref, out_ref):
    pa_count, row_count, bins, _, gates, element_count = samples_ref.shape
    tile = taps_ref.shape[1] // 2
    owners = tile // gates
    tiles_row = pa_count // owners

    def band(part):
        values = jnp.broadcast_to(taps_ref[part : part + 1, :], (tile, 2 * tile))
        return pltpu.roll(values, 0, 1, stride=1, stride_axis=0).astype(jnp.bfloat16)

    real_band, imag_band = band(0), band(1)
    own = jnp.concatenate([real_band[:, :tile], imag_band[:, :tile]], axis=1)
    before = jnp.concatenate([real_band[:, tile:], imag_band[:, tile:]], axis=1)
    bands = jnp.concatenate([own, before], axis=0)
    for b in range(bins):
        gram = jnp.zeros((2 * element_count, 2 * element_count), jnp.float32)
        carried = None
        for t in reversed(range(row_count * tiles_row)):
            row, first = t // tiles_row, t % tiles_row * owners
            real, imag = (
                samples_ref[first : first + owners, row, b, part].reshape(tile, element_count)
                for part in range(2)
            )
            upper = jnp.concatenate([real, imag], axis=1)
            lower = jnp.concatenate([-imag, real], axis=1)
            both = jnp.concatenate([upper, lower], axis=0)
            product = jnp.dot(bands, both, preferred_element_type=jnp.float32)
            filtered = product[:tile] if carried is None else product[:tile] + carried
            carried = product[tile:]
            filtered = filtered.astype(jnp.bfloat16)
            gram = gram + lax.dot_general(
                filtered, filtered, (((0,), (0,)), ((), ())), preferred_element_type=jnp.float32
            )
        n = element_count
        out_ref[b, 0] = (gram[:n, :n] + gram[n:, n:]) / total_gates
        out_ref[b, 1] = (gram[n:, :n] - gram[:n, n:]) / total_gates


def covariances(taps, samples, total_gates):
    bins, element_count = samples.shape[2], samples.shape[-1]
    return pl.pallas_call(
        functools.partial(covariance_kernel, total_gates),
        out_shape=jax.ShapeDtypeStruct((bins, 2, element_count, element_count), jnp.float32),
        in_specs=[pl.BlockSpec(memory_space=pltpu.VMEM)] * 2,
        out_specs=pl.BlockSpec(memory_space=pltpu.VMEM),
        compiler_params=pltpu.CompilerParams(vmem_limit_bytes=48 << 20),
        name="covariances",
    )(taps, samples)


def per_device(echoes, chirp_phase):
    gates_dev, pulses_dev, element_count = echoes.shape[1:]
    tap_count = chirp_phase.shape[0]
    pa_count, row_count = lax.axis_size("pa"), lax.axis_size("row")
    pulses, total_gates = pulses_dev * pa_count, gates_dev * row_count
    devices = pa_count * row_count
    gates = gates_dev // pa_count
    bins = pulses // devices
    taps = jnp.stack(filter_parts(chirp_phase)).astype(jnp.float32)
    taps = jnp.pad(taps, ((0, 0), (0, tap_count)))
    blocks = echoes.reshape(2, pa_count, gates, pulses_dev, element_count).swapaxes(0, 1)
    turned = lax.all_to_all(blocks, "pa", split_axis=0, concat_axis=0, tiled=True)
    spectrum = doppler(jnp.asarray(doppler_matrix(pulses)), turned)
    spectrum = spectrum.reshape(devices, bins, 2, gates, element_count)
    owned = lax.all_to_all(spectrum, ("pa", "row"), split_axis=0, concat_axis=0, tiled=True)
    owned = owned.reshape(pa_count, row_count, bins, 2, gates, element_count)
    return covariances(taps, owned, total_gates)


def solution(mesh):
    placed = (P(None, "row", "pa", None), P())
    return jax.shard_map(
        per_device,
        mesh=mesh,
        in_specs=placed,
        out_specs=P(("pa", "row"), None, None, None),
        check_vma=False,
    )
```

```python
import functools
import math

import jax
import jax.numpy as jnp
import numpy as np
from jax import lax
from jax.experimental import pallas as pl
from jax.experimental.pallas import tpu as pltpu
from jax.sharding import PartitionSpec as P


def doppler_matrix(pulses):
    indices = np.arange(pulses)
    products = indices[:, None] * indices[None, :] % pulses
    angles = (np.float32(2.0 * math.pi / pulses) * products.astype(np.float32)).astype(np.float64)
    scaling = 1.0 / math.sqrt(pulses)
    real_part = (np.cos(angles) * scaling).astype(np.float32)
    imag_part = (-np.sin(angles) * scaling).astype(np.float32)
    upper_half = np.stack([real_part, -imag_part], axis=1)
    lower_half = np.stack([imag_part, real_part], axis=1)
    matrix = np.stack([upper_half, lower_half], axis=1)
    return matrix.reshape(2 * pulses, 2 * pulses).astype(jnp.bfloat16)


def doppler_kernel(matrix_ref, samples_ref, out_ref, scratch):
    rows = matrix_ref.shape[0]
    gates, element_count = out_ref.shape[1:]
    matrix = matrix_ref[...]

    def columns(gate):
        parts = [samples_ref[:, part, gate].reshape(-1, element_count) for part in range(2)]
        return jnp.concatenate(parts, axis=0)

    for gate in range(0, gates, 2):
        both = jnp.concatenate([columns(gate), columns(gate + 1)], axis=1)
        product = jnp.dot(matrix, both, preferred_element_type=jnp.float32)
        for k in range(2):
            scratch[gate + k] = product[:, k * element_count : (k + 1) * element_count]
    step = 32
    for row in range(0, rows, step):
        block = scratch[:, row : row + step, :]
        out_ref[row : row + step] = jnp.transpose(block, (1, 0, 2)).astype(jnp.bfloat16)


def doppler(matrix, samples):
    owners, _, gates, pulses_dev, element_count = samples.shape
    rows = matrix.shape[0]
    block = math.gcd(16, gates)
    return pl.pallas_call(
        doppler_kernel,
        out_shape=jax.ShapeDtypeStruct((rows, gates, element_count), jnp.bfloat16),
        grid=(gates // block,),
        in_specs=[
            pl.BlockSpec(matrix.shape, lambda i: (0, 0)),
            pl.BlockSpec(
                (owners, 2, block, pulses_dev, element_count), lambda i: (0, 0, i, 0, 0)
            ),
        ],
        out_specs=pl.BlockSpec((rows, block, element_count), lambda i: (0, i, 0)),
        scratch_shapes=[pltpu.VMEM((block, rows, element_count), jnp.float32)],
        compiler_params=pltpu.CompilerParams(vmem_limit_bytes=20 << 20),
        name="doppler",
    )(matrix, samples)


def covariance_kernel(total_gates, phase_ref, samples_ref, out_ref):
    pa_count, row_count, _, _, gates, element_count = samples_ref.shape
    tile = phase_ref.shape[1]
    owners = tile // gates
    tiles_row = pa_count // owners
    scaling = 1.0 / math.sqrt(tile)

    def band(values):
        values = (values * scaling).astype(jnp.bfloat16).astype(jnp.float32)
        values = jnp.concatenate([values, jnp.zeros_like(values)], axis=1)
        values = jnp.broadcast_to(values, (tile, 2 * tile))
        return pltpu.roll(values, 0, 1, stride=1, stride_axis=0).astype(jnp.bfloat16)

    real_band, imag_band = band(jnp.cos(phase_ref[...])), band(-jnp.sin(phase_ref[...]))
    own = jnp.concatenate([real_band[:, :tile], imag_band[:, :tile]], axis=1)
    before = jnp.concatenate([real_band[:, tile:], imag_band[:, tile:]], axis=1)
    bands = jnp.concatenate([own, before], axis=0)
    n = element_count
    gram = jnp.zeros((2 * n, 2 * n), jnp.float32)
    carried = None
    for t in reversed(range(row_count * tiles_row)):
        row, first = t // tiles_row, t % tiles_row * owners
        real, imag = (
            samples_ref[first : first + owners, row, 0, part].reshape(tile, n) for part in range(2)
        )
        upper = jnp.concatenate([real, imag], axis=1)
        lower = jnp.concatenate([-imag, real], axis=1)
        both = jnp.concatenate([upper, lower], axis=0)
        product = jnp.dot(bands, both, preferred_element_type=jnp.float32)
        filtered = product[:tile] if carried is None else product[:tile] + carried
        carried = product[tile:]
        filtered = filtered.astype(jnp.bfloat16)
        gram = gram + lax.dot_general(
            filtered, filtered, (((0,), (0,)), ((), ())), preferred_element_type=jnp.float32
        )
    out_ref[0, 0] = (gram[:n, :n] + gram[n:, n:]) / total_gates
    out_ref[0, 1] = (gram[n:, :n] - gram[:n, n:]) / total_gates


def covariances(phase, samples, total_gates):
    pa_count, row_count, bins, _, gates, element_count = samples.shape
    return pl.pallas_call(
        functools.partial(covariance_kernel, total_gates),
        out_shape=jax.ShapeDtypeStruct((bins, 2, element_count, element_count), jnp.float32),
        grid=(bins,),
        in_specs=[
            pl.BlockSpec(phase.shape, lambda b: (0, 0)),
            pl.BlockSpec(
                (pa_count, row_count, 1, 2, gates, element_count), lambda b: (0, 0, b, 0, 0, 0)
            ),
        ],
        out_specs=pl.BlockSpec((1, 2, element_count, element_count), lambda b: (b, 0, 0, 0)),
        compiler_params=pltpu.CompilerParams(vmem_limit_bytes=20 << 20),
        name="covariances",
    )(phase, samples)


def per_device(echoes, chirp_phase):
    gates_dev, pulses_dev, element_count = echoes.shape[1:]
    pa_count, row_count = lax.axis_size("pa"), lax.axis_size("row")
    pulses, total_gates = pulses_dev * pa_count, gates_dev * row_count
    devices = pa_count * row_count
    gates = gates_dev // pa_count
    bins = pulses // devices
    blocks = echoes.reshape(2, pa_count, gates, pulses_dev, element_count).swapaxes(0, 1)
    turned = lax.all_to_all(blocks, "pa", split_axis=0, concat_axis=0, tiled=True)
    spectrum = doppler(jnp.asarray(doppler_matrix(pulses)), turned)
    spectrum = spectrum.reshape(devices, bins, 2, gates, element_count)
    owned = lax.all_to_all(spectrum, ("pa", "row"), split_axis=0, concat_axis=0, tiled=True)
    owned = owned.reshape(pa_count, row_count, bins, 2, gates, element_count)
    return covariances(chirp_phase[None], owned, total_gates)


def solution(mesh):
    placed = (P(None, "row", "pa", None), P())
    return jax.shard_map(
        per_device,
        mesh=mesh,
        in_specs=placed,
        out_specs=P(("pa", "row"), None, None, None),
        check_vma=False,
    )
```

```python
import functools
import math

import jax
import jax.numpy as jnp
import numpy as np
from jax import lax
from jax.experimental import pallas as pl
from jax.experimental.pallas import tpu as pltpu
from jax.sharding import PartitionSpec as P


def doppler_matrix(pulses):
    indices = np.arange(pulses)
    products = indices[:, None] * indices[None, :] % pulses
    angles = (np.float32(2.0 * math.pi / pulses) * products.astype(np.float32)).astype(np.float64)
    scaling = 1.0 / math.sqrt(pulses)
    real_part = (np.cos(angles) * scaling).astype(np.float32)
    imag_part = (-np.sin(angles) * scaling).astype(np.float32)
    upper_half = np.stack([real_part, -imag_part], axis=1)
    lower_half = np.stack([imag_part, real_part], axis=1)
    matrix = np.stack([upper_half, lower_half], axis=1)
    return matrix.reshape(2 * pulses, 2 * pulses).astype(jnp.bfloat16)


def doppler_kernel(matrix_ref, samples_ref, out_ref, scratch):
    rows = matrix_ref.shape[0]
    gates, element_count = out_ref.shape[1:]
    slots, group = scratch.shape[:2]

    def columns(gate):
        parts = [samples_ref[:, part, gate].reshape(-1, element_count) for part in range(2)]
        return jnp.concatenate(parts, axis=0)

    step = 32
    for first in range(0, gates, group):
        slot = first // group % slots
        for k in range(0, group, 2):
            both = jnp.concatenate([columns(first + k), columns(first + k + 1)], axis=1)
            product = jnp.dot(matrix_ref[...], both, preferred_element_type=jnp.float32)
            scratch[slot, k] = product[:, :element_count]
            scratch[slot, k + 1] = product[:, element_count:]
        for row in range(0, rows, step):
            block = jnp.transpose(scratch[slot, :, row : row + step, :], (1, 0, 2))
            out_ref[row : row + step, first : first + group] = block.astype(jnp.bfloat16)


def doppler(matrix, samples):
    gates, _, element_count = samples.shape[2:]
    rows = matrix.shape[0]
    group = math.gcd(16, gates)
    return pl.pallas_call(
        doppler_kernel,
        out_shape=jax.ShapeDtypeStruct((rows, gates, element_count), jnp.bfloat16),
        in_specs=[pl.BlockSpec(memory_space=pltpu.VMEM)] * 2,
        out_specs=pl.BlockSpec(memory_space=pltpu.VMEM),
        scratch_shapes=[pltpu.VMEM((2, group, rows, element_count), jnp.float32)],
        compiler_params=pltpu.CompilerParams(vmem_limit_bytes=24 << 20),
        name="doppler",
    )(matrix, samples)


def covariance_kernel(total_gates, phase_ref, samples_ref, out_ref):
    pa_count, row_count, _, _, gates, n = samples_ref.shape
    b = pl.program_id(0)
    taps = phase_ref.shape[1]
    reach = 2
    tile = taps // reach
    owners = tile // gates
    tiles_row = pa_count // owners
    scaling = 1.0 / math.sqrt(taps)

    def band(values):
        values = (values * scaling).astype(jnp.bfloat16).astype(jnp.float32)
        values = jnp.concatenate([values, jnp.zeros((1, tile), jnp.float32)], axis=1)
        values = jnp.broadcast_to(values, (tile, taps + tile))
        return pltpu.roll(values, 0, 1, stride=1, stride_axis=0).astype(jnp.bfloat16)

    real_band, imag_band = band(jnp.cos(phase_ref[...])), band(-jnp.sin(phase_ref[...]))
    parts = [slice(k * tile, (k + 1) * tile) for k in range(reach + 1)]
    bands = [jnp.concatenate([real_band[:, k], imag_band[:, k]], axis=1) for k in parts]
    bands = jnp.concatenate(bands, axis=0)
    gram = jnp.zeros((2 * n, 2 * n), jnp.float32)
    carried = [None] * reach
    waiting = []
    for t in reversed(range(row_count * tiles_row)):
        row, first = t // tiles_row, t % tiles_row * owners
        real, imag = (
            samples_ref[first : first + owners, row, b, part].reshape(tile, n) for part in range(2)
        )
        upper = jnp.concatenate([real, imag], axis=1)
        lower = jnp.concatenate([-imag, real], axis=1)
        both = jnp.concatenate([upper, lower], axis=0)
        product = jnp.dot(bands, both, preferred_element_type=jnp.float32)
        sums = [product[k] for k in parts]
        sums = [x if y is None else x + y for x, y in zip(sums, carried + [None])]
        carried = sums[1:]
        waiting.append(sums[0].astype(jnp.bfloat16))
        if len(waiting) == reach:
            filtered = jnp.concatenate(waiting, axis=0)
            waiting = []
            gram = gram + lax.dot_general(
                filtered, filtered, (((0,), (0,)), ((), ())), preferred_element_type=jnp.float32
            )
    out_ref[0, 0] = (gram[:n, :n] + gram[n:, n:]) / total_gates
    out_ref[0, 1] = (gram[n:, :n] - gram[:n, n:]) / total_gates


def covariances(phase, samples, total_gates):
    bins, element_count = samples.shape[2], samples.shape[-1]
    return pl.pallas_call(
        functools.partial(covariance_kernel, total_gates),
        out_shape=jax.ShapeDtypeStruct((bins, 2, element_count, element_count), jnp.float32),
        grid=(bins,),
        in_specs=[pl.BlockSpec(memory_space=pltpu.VMEM)] * 2,
        out_specs=pl.BlockSpec((1, 2, element_count, element_count), lambda b: (b, 0, 0, 0)),
        compiler_params=pltpu.CompilerParams(vmem_limit_bytes=20 << 20),
        name="covariances",
    )(phase, samples)


def per_device(echoes, chirp_phase):
    gates_dev, pulses_dev, element_count = echoes.shape[1:]
    pa_count, row_count = lax.axis_size("pa"), lax.axis_size("row")
    pulses, total_gates = pulses_dev * pa_count, gates_dev * row_count
    devices = pa_count * row_count
    gates = gates_dev // pa_count
    bins = pulses // devices
    blocks = echoes.reshape(2, pa_count, gates, pulses_dev, element_count).swapaxes(0, 1)
    turned = lax.all_to_all(blocks, "pa", split_axis=0, concat_axis=0, tiled=True)
    spectrum = doppler(jnp.asarray(doppler_matrix(pulses)), turned)
    spectrum = spectrum.reshape(devices, bins, 2, gates, element_count)
    owned = lax.all_to_all(spectrum, ("pa", "row"), split_axis=0, concat_axis=0, tiled=True)
    owned = owned.reshape(pa_count, row_count, bins, 2, gates, element_count)
    return covariances(chirp_phase[None], owned, total_gates)


def solution(mesh):
    placed = (P(None, "row", "pa", None), P())
    return jax.shard_map(
        per_device,
        mesh=mesh,
        in_specs=placed,
        out_specs=P(("pa", "row"), None, None, None),
        check_vma=False,
    )
```

```python
import functools
import math

import jax
import jax.numpy as jnp
import numpy as np
from jax import lax
from jax.experimental import pallas as pl
from jax.experimental.pallas import tpu as pltpu
from jax.sharding import PartitionSpec as P


def doppler_matrix(pulses):
    indices = np.arange(pulses)
    products = indices[:, None] * indices[None, :] % pulses
    angles = (np.float32(2.0 * math.pi / pulses) * products.astype(np.float32)).astype(np.float64)
    scaling = 1.0 / math.sqrt(pulses)
    real_part = (np.cos(angles) * scaling).astype(np.float32)
    imag_part = (-np.sin(angles) * scaling).astype(np.float32)
    upper_half = np.stack([real_part, -imag_part], axis=1)
    lower_half = np.stack([imag_part, real_part], axis=1)
    matrix = np.stack([upper_half, lower_half], axis=1)
    return matrix.reshape(2 * pulses, 2 * pulses).astype(jnp.bfloat16)


def doppler_kernel(matrix_ref, samples_ref, out_ref, scratch):
    rows = matrix_ref.shape[0]
    gates, element_count = out_ref.shape[1:]
    slots, group = scratch.shape[:2]

    def columns(gate):
        parts = [samples_ref[:, part, gate].reshape(-1, element_count) for part in range(2)]
        return jnp.concatenate(parts, axis=0)

    step = 32
    for first in range(0, gates, group):
        slot = first // group % slots
        for k in range(0, group, 2):
            both = jnp.concatenate([columns(first + k), columns(first + k + 1)], axis=1)
            product = jnp.dot(matrix_ref[...], both, preferred_element_type=jnp.float32)
            scratch[slot, k] = product[:, :element_count]
            scratch[slot, k + 1] = product[:, element_count:]
        for row in range(0, rows, step):
            block = jnp.transpose(scratch[slot, :, row : row + step, :], (1, 0, 2))
            out_ref[row : row + step, first : first + group] = block.astype(jnp.bfloat16)


def doppler(matrix, samples):
    gates, _, element_count = samples.shape[2:]
    rows = matrix.shape[0]
    group = math.gcd(16, gates)
    return pl.pallas_call(
        doppler_kernel,
        out_shape=jax.ShapeDtypeStruct((rows, gates, element_count), jnp.bfloat16),
        in_specs=[pl.BlockSpec(memory_space=pltpu.VMEM)] * 2,
        out_specs=pl.BlockSpec(memory_space=pltpu.VMEM),
        scratch_shapes=[pltpu.VMEM((2, group, rows, element_count), jnp.float32)],
        compiler_params=pltpu.CompilerParams(vmem_limit_bytes=24 << 20),
        name="doppler",
    )(matrix, samples)


def repack_kernel(echoes_ref, out_ref, sems):
    owners = out_ref.shape[0]
    step = owners // sems.shape[1]
    copies = [
        pltpu.make_async_copy(
            echoes_ref.at[part, pl.ds(k * step, step)],
            out_ref.at[pl.ds(k * step, step), part],
            sems.at[part, k],
        )
        for part in range(2)
        for k in range(sems.shape[1])
    ]
    for copy in copies:
        copy.start()
    for copy in copies:
        copy.wait()


def repack(echoes):
    shape = (echoes.shape[1], 2) + echoes.shape[2:]
    return pl.pallas_call(
        repack_kernel,
        out_shape=jax.ShapeDtypeStruct(shape, echoes.dtype),
        in_specs=[pl.BlockSpec(memory_space=pltpu.HBM)],
        out_specs=pl.BlockSpec(memory_space=pltpu.VMEM),
        scratch_shapes=[pltpu.SemaphoreType.DMA((2, 4))],
        compiler_params=pltpu.CompilerParams(vmem_limit_bytes=8 << 20),
        name="repack",
    )(echoes)


def covariance_kernel(total_gates, phase_ref, samples_ref, out_ref):
    pa_count, row_count, _, _, gates, n = samples_ref.shape
    b = pl.program_id(0)
    taps = phase_ref.shape[1]
    reach = 2
    tile = taps // reach
    owners = tile // gates
    tiles_row = pa_count // owners
    scaling = 1.0 / math.sqrt(taps)

    def band(values):
        values = (values * scaling).astype(jnp.bfloat16).astype(jnp.float32)
        values = jnp.concatenate([values, jnp.zeros((1, tile), jnp.float32)], axis=1)
        values = jnp.broadcast_to(values, (tile, taps + tile))
        return pltpu.roll(values, 0, 1, stride=1, stride_axis=0).astype(jnp.bfloat16)

    real_band, imag_band = band(jnp.cos(phase_ref[...])), band(-jnp.sin(phase_ref[...]))
    parts = [slice(k * tile, (k + 1) * tile) for k in range(reach + 1)]
    bands = [jnp.concatenate([real_band[:, k], imag_band[:, k]], axis=1) for k in parts]
    bands = jnp.concatenate(bands, axis=0)
    gram = jnp.zeros((2 * n, 2 * n), jnp.float32)
    carried = [None] * reach
    waiting = []
    for t in reversed(range(row_count * tiles_row)):
        row, first = t // tiles_row, t % tiles_row * owners
        real, imag = (
            samples_ref[first : first + owners, row, b, part].reshape(tile, n) for part in range(2)
        )
        upper = jnp.concatenate([real, imag], axis=1)
        lower = jnp.concatenate([-imag, real], axis=1)
        both = jnp.concatenate([upper, lower], axis=0)
        product = jnp.dot(bands, both, preferred_element_type=jnp.float32)
        sums = [product[k] for k in parts]
        sums = [x if y is None else x + y for x, y in zip(sums, carried + [None])]
        carried = sums[1:]
        waiting.append(sums[0].astype(jnp.bfloat16))
        if len(waiting) == 4 * reach:
            filtered = jnp.concatenate(waiting, axis=0)
            waiting = []
            gram = gram + lax.dot_general(
                filtered, filtered, (((0,), (0,)), ((), ())), preferred_element_type=jnp.float32
            )
    out_ref[0, 0] = (gram[:n, :n] + gram[n:, n:]) / total_gates
    out_ref[0, 1] = (gram[n:, :n] - gram[:n, n:]) / total_gates


def covariances(phase, samples, total_gates):
    bins, element_count = samples.shape[2], samples.shape[-1]
    return pl.pallas_call(
        functools.partial(covariance_kernel, total_gates),
        out_shape=jax.ShapeDtypeStruct((bins, 2, element_count, element_count), jnp.float32),
        grid=(bins,),
        in_specs=[pl.BlockSpec(memory_space=pltpu.VMEM)] * 2,
        out_specs=pl.BlockSpec((1, 2, element_count, element_count), lambda b: (b, 0, 0, 0)),
        compiler_params=pltpu.CompilerParams(vmem_limit_bytes=20 << 20),
        name="covariances",
    )(phase, samples)


def per_device(echoes, chirp_phase):
    gates_dev, pulses_dev, element_count = echoes.shape[1:]
    pa_count, row_count = lax.axis_size("pa"), lax.axis_size("row")
    pulses, total_gates = pulses_dev * pa_count, gates_dev * row_count
    devices = pa_count * row_count
    gates = gates_dev // pa_count
    bins = pulses // devices
    blocks = echoes.reshape(2, pa_count, gates, pulses_dev, element_count)
    blocks = repack(pltpu.with_memory_space_constraint(blocks, pltpu.HBM))
    turned = lax.all_to_all(blocks, "pa", split_axis=0, concat_axis=0, tiled=True)
    spectrum = doppler(jnp.asarray(doppler_matrix(pulses)), turned)
    spectrum = spectrum.reshape(devices, bins, 2, gates, element_count)
    owned = lax.all_to_all(spectrum, ("pa", "row"), split_axis=0, concat_axis=0, tiled=True)
    owned = owned.reshape(pa_count, row_count, bins, 2, gates, element_count)
    return covariances(chirp_phase[None], owned, total_gates)


def solution(mesh):
    placed = (P(None, "row", "pa", None), P())
    return jax.shard_map(
        per_device,
        mesh=mesh,
        in_specs=placed,
        out_specs=P(("pa", "row"), None, None, None),
        check_vma=False,
    )
```

```python
import functools
import math

import jax
import jax.numpy as jnp
import numpy as np
from jax import lax
from jax.experimental import pallas as pl
from jax.experimental.pallas import tpu as pltpu
from jax.sharding import PartitionSpec as P


def doppler_matrix(pulses):
    indices = np.arange(pulses)
    products = indices[:, None] * indices[None, :] % pulses
    angles = (np.float32(2.0 * math.pi / pulses) * products.astype(np.float32)).astype(np.float64)
    scaling = 1.0 / math.sqrt(pulses)
    real_part = (np.cos(angles) * scaling).astype(np.float32)
    imag_part = (-np.sin(angles) * scaling).astype(np.float32)
    upper_half = np.stack([real_part, -imag_part], axis=1)
    lower_half = np.stack([imag_part, real_part], axis=1)
    matrix = np.stack([upper_half, lower_half], axis=1)
    return matrix.reshape(2 * pulses, 2 * pulses).astype(jnp.bfloat16)


def doppler_kernel(matrix_ref, samples_ref, out_ref, scratch):
    rows = matrix_ref.shape[0]
    gates, element_count = out_ref.shape[1:]
    slots, group = scratch.shape[:2]

    def columns(gate):
        parts = [samples_ref[:, part, gate].reshape(-1, element_count) for part in range(2)]
        return jnp.concatenate(parts, axis=0)

    step = 32
    for first in range(0, gates, group):
        slot = first // group % slots
        for k in range(0, group, 2):
            both = jnp.concatenate([columns(first + k), columns(first + k + 1)], axis=1)
            product = jnp.dot(matrix_ref[...], both, preferred_element_type=jnp.float32)
            scratch[slot, k] = product[:, :element_count]
            scratch[slot, k + 1] = product[:, element_count:]
        for row in range(0, rows, step):
            block = jnp.transpose(scratch[slot, :, row : row + step, :], (1, 0, 2))
            out_ref[row : row + step, first : first + group] = block.astype(jnp.bfloat16)


def doppler(matrix, samples):
    gates, _, element_count = samples.shape[2:]
    rows = matrix.shape[0]
    group = math.gcd(16, gates)
    return pl.pallas_call(
        doppler_kernel,
        out_shape=jax.ShapeDtypeStruct((rows, gates, element_count), jnp.bfloat16),
        in_specs=[pl.BlockSpec(memory_space=pltpu.VMEM)] * 2,
        out_specs=pl.BlockSpec(memory_space=pltpu.VMEM),
        scratch_shapes=[pltpu.VMEM((2, group, rows, element_count), jnp.float32)],
        compiler_params=pltpu.CompilerParams(vmem_limit_bytes=24 << 20),
        name="doppler",
    )(matrix, samples)


def repack_kernel(echoes_ref, out_ref, sems):
    owners = out_ref.shape[0]
    step = owners // sems.shape[1]
    copies = [
        pltpu.make_async_copy(
            echoes_ref.at[part, pl.ds(k * step, step)],
            out_ref.at[pl.ds(k * step, step), part],
            sems.at[part, k],
        )
        for part in range(2)
        for k in range(sems.shape[1])
    ]
    for copy in copies:
        copy.start()
    for copy in copies:
        copy.wait()


def repack(echoes):
    shape = (echoes.shape[1], 2) + echoes.shape[2:]
    return pl.pallas_call(
        repack_kernel,
        out_shape=jax.ShapeDtypeStruct(shape, echoes.dtype),
        in_specs=[pl.BlockSpec(memory_space=pltpu.HBM)],
        out_specs=pl.BlockSpec(memory_space=pltpu.VMEM),
        scratch_shapes=[pltpu.SemaphoreType.DMA((2, 4))],
        compiler_params=pltpu.CompilerParams(vmem_limit_bytes=8 << 20),
        name="repack",
    )(echoes)


def covariance_kernel(total_gates, phase_ref, samples_ref, out_ref):
    pa_count, row_count, bins, _, gates, n = samples_ref.shape
    taps = phase_ref.shape[1]
    reach = 2
    tile = taps // reach
    owners = tile // gates
    tiles_row = pa_count // owners
    scaling = 1.0 / math.sqrt(taps)

    def band(values):
        values = (values * scaling).astype(jnp.bfloat16).astype(jnp.float32)
        values = jnp.concatenate([values, jnp.zeros((1, tile), jnp.float32)], axis=1)
        values = jnp.broadcast_to(values, (tile, taps + tile))
        return pltpu.roll(values, 0, 1, stride=1, stride_axis=0).astype(jnp.bfloat16)

    real_band, imag_band = band(jnp.cos(phase_ref[...])), band(-jnp.sin(phase_ref[...]))
    parts = [slice(k * tile, (k + 1) * tile) for k in range(reach + 1)]
    bands = [jnp.concatenate([real_band[:, k], imag_band[:, k]], axis=1) for k in parts]
    bands = jnp.concatenate(bands, axis=0)
    carried = [None] * reach
    filtered = []
    for t in reversed(range(row_count * tiles_row)):
        row, first = t // tiles_row, t % tiles_row * owners
        columns = []
        for b in range(bins):
            real, imag = (
                samples_ref[first : first + owners, row, b, part].reshape(tile, n) for part in range(2)
            )
            upper = jnp.concatenate([real, imag], axis=1)
            lower = jnp.concatenate([-imag, real], axis=1)
            columns.append(jnp.concatenate([upper, lower], axis=0))
        columns = jnp.concatenate(columns, axis=1)
        product = jnp.dot(bands, columns, preferred_element_type=jnp.float32)
        sums = [product[k] for k in parts]
        sums = [x if y is None else x + y for x, y in zip(sums, carried + [None])]
        carried = sums[1:]
        filtered.append(sums[0].astype(jnp.bfloat16))
    filtered = jnp.concatenate(filtered, axis=0)
    for b in range(bins):
        one = filtered[:, b * 2 * n : (b + 1) * 2 * n]
        gram = lax.dot_general(
            one, one, (((0,), (0,)), ((), ())), preferred_element_type=jnp.float32
        )
        out_ref[b, 0] = (gram[:n, :n] + gram[n:, n:]) / total_gates
        out_ref[b, 1] = (gram[n:, :n] - gram[:n, n:]) / total_gates


def covariances(phase, samples, total_gates):
    bins, element_count = samples.shape[2], samples.shape[-1]
    return pl.pallas_call(
        functools.partial(covariance_kernel, total_gates),
        out_shape=jax.ShapeDtypeStruct((bins, 2, element_count, element_count), jnp.float32),
        in_specs=[pl.BlockSpec(memory_space=pltpu.VMEM)] * 2,
        out_specs=pl.BlockSpec(memory_space=pltpu.VMEM),
        compiler_params=pltpu.CompilerParams(vmem_limit_bytes=24 << 20),
        name="covariances",
    )(phase, samples)


def per_device(echoes, chirp_phase):
    gates_dev, pulses_dev, element_count = echoes.shape[1:]
    pa_count, row_count = lax.axis_size("pa"), lax.axis_size("row")
    pulses, total_gates = pulses_dev * pa_count, gates_dev * row_count
    devices = pa_count * row_count
    gates = gates_dev // pa_count
    bins = pulses // devices
    blocks = echoes.reshape(2, pa_count, gates, pulses_dev, element_count)
    blocks = repack(pltpu.with_memory_space_constraint(blocks, pltpu.HBM))
    turned = lax.all_to_all(blocks, "pa", split_axis=0, concat_axis=0, tiled=True)
    spectrum = doppler(jnp.asarray(doppler_matrix(pulses)), turned)
    spectrum = spectrum.reshape(devices, bins, 2, gates, element_count)
    owned = lax.all_to_all(spectrum, ("pa", "row"), split_axis=0, concat_axis=0, tiled=True)
    owned = owned.reshape(pa_count, row_count, bins, 2, gates, element_count)
    return covariances(chirp_phase[None], owned, total_gates)


def solution(mesh):
    placed = (P(None, "row", "pa", None), P())
    return jax.shard_map(
        per_device,
        mesh=mesh,
        in_specs=placed,
        out_specs=P(("pa", "row"), None, None, None),
        check_vma=False,
    )
```

```python
import functools
import math

import jax
import jax.numpy as jnp
import numpy as np
from jax import lax
from jax.experimental import pallas as pl
from jax.experimental.pallas import tpu as pltpu
from jax.sharding import PartitionSpec as P


def doppler_rows(pulses):
    half = pulses // 2
    products = np.arange(half + 1)[:, None] * np.arange(pulses)[None, :] % pulses
    angles = (np.float32(2.0 * math.pi / pulses) * products.astype(np.float32)).astype(np.float64)
    scaling = 1.0 / math.sqrt(pulses)
    rows = np.concatenate([np.cos(angles), np.sin(angles[1:half])], axis=0) * scaling
    return rows.astype(np.float32).astype(jnp.bfloat16)


def doppler_kernel(rows_ref, samples_ref, out_ref, scratch):
    pulses = rows_ref.shape[0]
    half = pulses // 2
    gates, n = out_ref.shape[1:]
    slots, _, group = scratch.shape[:3]
    step = 8
    top = lax.broadcasted_iota(jnp.int32, (step, n), 0) == 0

    def turn(first, slot, low, high):
        for kind in range(4):
            for row in range(low, high, step):
                block = jnp.transpose(scratch[slot, kind, :, row : row + step, :], (1, 0, 2))
                block = block.astype(jnp.bfloat16)
                for j in range(step):
                    b = row + j
                    if kind >= 2:
                        b = pulses - b if b else half
                    out_ref[2 * b + kind % 2, first : first + group] = block[j]

    for first in range(0, gates, group):
        slot = first // group % slots
        for k in range(group):
            parts = [samples_ref[:, part, first + k].reshape(-1, n) for part in range(2)]
            product = jnp.dot(
                rows_ref[...], jnp.concatenate(parts, axis=1), preferred_element_type=jnp.float32
            )
            cos_real, cos_imag = product[:half, :n], product[:half, n:]
            sin_real, sin_imag = product[half:, :n], product[half:, n:]
            values = (
                cos_real + sin_imag,
                cos_imag - sin_real,
                cos_real - sin_imag,
                cos_imag + sin_real,
            )
            tops = (cos_real, cos_imag, sin_real, sin_imag)
            for kind in range(4):
                scratch[slot, kind, k] = values[kind]
                scratch[slot, kind, k, :step] = jnp.where(top, tops[kind][:step], values[kind][:step])
            if first:
                turn(first - group, 1 - slot, half * k // group, half * (k + 1) // group)
    turn(gates - group, (gates // group - 1) % slots, 0, half)


def doppler(rows, samples):
    gates, _, n = samples.shape[2:]
    pulses = rows.shape[0]
    group = math.gcd(16, gates)
    return pl.pallas_call(
        doppler_kernel,
        out_shape=jax.ShapeDtypeStruct((2 * pulses, gates, n), jnp.bfloat16),
        in_specs=[pl.BlockSpec(memory_space=pltpu.VMEM)] * 2,
        out_specs=pl.BlockSpec(memory_space=pltpu.VMEM),
        scratch_shapes=[pltpu.VMEM((2, 4, group, pulses // 2, n), jnp.float32)],
        compiler_params=pltpu.CompilerParams(vmem_limit_bytes=24 << 20),
        name="doppler",
    )(rows, samples)


def repack_kernel(echoes_ref, out_ref, sems):
    owners = out_ref.shape[0]
    step = owners // sems.shape[1]
    copies = [
        pltpu.make_async_copy(
            echoes_ref.at[part, pl.ds(k * step, step)],
            out_ref.at[pl.ds(k * step, step), part],
            sems.at[part, k],
        )
        for part in range(2)
        for k in range(sems.shape[1])
    ]
    for copy in copies:
        copy.start()
    for copy in copies:
        copy.wait()


def repack(echoes):
    shape = (echoes.shape[1], 2) + echoes.shape[2:]
    return pl.pallas_call(
        repack_kernel,
        out_shape=jax.ShapeDtypeStruct(shape, echoes.dtype),
        in_specs=[pl.BlockSpec(memory_space=pltpu.HBM)],
        out_specs=pl.BlockSpec(memory_space=pltpu.VMEM),
        scratch_shapes=[pltpu.SemaphoreType.DMA((2, 4))],
        compiler_params=pltpu.CompilerParams(vmem_limit_bytes=8 << 20),
        name="repack",
    )(echoes)


def covariance_kernel(total_gates, phase_ref, samples_ref, out_ref):
    pa_count, row_count, bins, _, gates, n = samples_ref.shape
    taps = phase_ref.shape[1]
    reach = 2
    tile = taps // reach
    owners = tile // gates
    tiles_row = pa_count // owners
    scaling = 1.0 / math.sqrt(taps)

    def band(values):
        values = (values * scaling).astype(jnp.bfloat16).astype(jnp.float32)
        values = jnp.concatenate([values, jnp.zeros((1, tile), jnp.float32)], axis=1)
        values = jnp.broadcast_to(values, (tile, taps + tile))
        return pltpu.roll(values, 0, 1, stride=1, stride_axis=0).astype(jnp.bfloat16)

    real_band, imag_band = band(jnp.cos(phase_ref[...])), band(-jnp.sin(phase_ref[...]))
    parts = [slice(k * tile, (k + 1) * tile) for k in range(reach + 1)]
    bands = [jnp.concatenate([real_band[:, k], imag_band[:, k]], axis=1) for k in parts]
    bands = jnp.concatenate(bands, axis=0)
    carried = [None] * reach
    filtered = []
    for t in reversed(range(row_count * tiles_row)):
        row, first = t // tiles_row, t % tiles_row * owners
        columns = []
        for b in range(bins):
            real, imag = (
                samples_ref[first : first + owners, row, b, part].reshape(tile, n) for part in range(2)
            )
            upper = jnp.concatenate([real, imag], axis=1)
            lower = jnp.concatenate([-imag, real], axis=1)
            columns.append(jnp.concatenate([upper, lower], axis=0))
        columns = jnp.concatenate(columns, axis=1)
        product = jnp.dot(bands, columns, preferred_element_type=jnp.float32)
        sums = [product[k] for k in parts]
        sums = [x if y is None else x + y for x, y in zip(sums, carried + [None])]
        carried = sums[1:]
        filtered.append(sums[0].astype(jnp.bfloat16))
    filtered = jnp.concatenate(filtered, axis=0)
    for b in range(bins):
        one = filtered[:, b * 2 * n : (b + 1) * 2 * n]
        gram = lax.dot_general(
            one, one, (((0,), (0,)), ((), ())), preferred_element_type=jnp.float32
        )
        out_ref[b, 0] = (gram[:n, :n] + gram[n:, n:]) / total_gates
        out_ref[b, 1] = (gram[n:, :n] - gram[:n, n:]) / total_gates


def covariances(phase, samples, total_gates):
    bins, element_count = samples.shape[2], samples.shape[-1]
    return pl.pallas_call(
        functools.partial(covariance_kernel, total_gates),
        out_shape=jax.ShapeDtypeStruct((bins, 2, element_count, element_count), jnp.float32),
        in_specs=[pl.BlockSpec(memory_space=pltpu.VMEM)] * 2,
        out_specs=pl.BlockSpec(memory_space=pltpu.VMEM),
        compiler_params=pltpu.CompilerParams(vmem_limit_bytes=24 << 20),
        name="covariances",
    )(phase, samples)


def per_device(echoes, chirp_phase):
    gates_dev, pulses_dev, element_count = echoes.shape[1:]
    pa_count, row_count = lax.axis_size("pa"), lax.axis_size("row")
    pulses, total_gates = pulses_dev * pa_count, gates_dev * row_count
    devices = pa_count * row_count
    gates = gates_dev // pa_count
    bins = pulses // devices
    blocks = echoes.reshape(2, pa_count, gates, pulses_dev, element_count)
    blocks = repack(pltpu.with_memory_space_constraint(blocks, pltpu.HBM))
    turned = lax.all_to_all(blocks, "pa", split_axis=0, concat_axis=0, tiled=True)
    spectrum = doppler(jnp.asarray(doppler_rows(pulses)), turned)
    spectrum = spectrum.reshape(devices, bins, 2, gates, element_count)
    owned = lax.all_to_all(spectrum, ("pa", "row"), split_axis=0, concat_axis=0, tiled=True)
    owned = owned.reshape(pa_count, row_count, bins, 2, gates, element_count)
    return covariances(chirp_phase[None], owned, total_gates)


def solution(mesh):
    placed = (P(None, "row", "pa", None), P())
    return jax.shard_map(
        per_device,
        mesh=mesh,
        in_specs=placed,
        out_specs=P(("pa", "row"), None, None, None),
        check_vma=False,
    )
```

```python
import functools
import math

import jax
import jax.numpy as jnp
import numpy as np
from jax import lax
from jax.experimental import pallas as pl
from jax.experimental.pallas import tpu as pltpu
from jax.sharding import Mesh
from jax.sharding import PartitionSpec as P


PA = ("xl", "y", "core")
ROW = ("z", "xh")
EXCHANGE = ("z", "y", "xh", "xl", "core")


def doppler_rows(pulses):
    half = pulses // 2
    products = np.arange(half + 1)[:, None] * np.arange(pulses)[None, :] % pulses
    angles = (np.float32(2.0 * math.pi / pulses) * products.astype(np.float32)).astype(np.float64)
    scaling = 1.0 / math.sqrt(pulses)
    rows = np.concatenate([np.cos(angles), np.sin(angles[1:half])], axis=0) * scaling
    return rows.astype(np.float32).astype(jnp.bfloat16)


def doppler_kernel(places, rows_ref, samples_ref, out_ref, scratch):
    pulses = rows_ref.shape[0]
    half = pulses // 2
    gates, n = out_ref.shape[1:]
    slots, _, group = scratch.shape[:3]
    step = 8
    top = lax.broadcasted_iota(jnp.int32, (step, n), 0) == 0

    def turn(first, slot, low, high):
        for kind in range(4):
            for row in range(low, high, step):
                block = jnp.transpose(scratch[slot, kind, :, row : row + step, :], (1, 0, 2))
                block = block.astype(jnp.bfloat16)
                for j in range(step):
                    b = row + j
                    if kind >= 2:
                        b = pulses - b if b else half
                    out_ref[2 * places[b] + kind % 2, first : first + group] = block[j]

    for first in range(0, gates, group):
        slot = first // group % slots
        for k in range(group):
            parts = [samples_ref[:, part, first + k].reshape(-1, n) for part in range(2)]
            product = jnp.dot(
                rows_ref[...], jnp.concatenate(parts, axis=1), preferred_element_type=jnp.float32
            )
            cos_real, cos_imag = product[:half, :n], product[:half, n:]
            sin_real, sin_imag = product[half:, :n], product[half:, n:]
            values = (
                cos_real + sin_imag,
                cos_imag - sin_real,
                cos_real - sin_imag,
                cos_imag + sin_real,
            )
            tops = (cos_real, cos_imag, sin_real, sin_imag)
            for kind in range(4):
                scratch[slot, kind, k] = values[kind]
                scratch[slot, kind, k, :step] = jnp.where(top, tops[kind][:step], values[kind][:step])
            if first:
                turn(first - group, 1 - slot, half * k // group, half * (k + 1) // group)
    turn(gates - group, (gates // group - 1) % slots, 0, half)


def doppler(rows, samples, places):
    gates, _, n = samples.shape[2:]
    pulses = rows.shape[0]
    group = math.gcd(16, gates)
    return pl.pallas_call(
        functools.partial(doppler_kernel, places),
        out_shape=jax.ShapeDtypeStruct((2 * pulses, gates, n), jnp.bfloat16),
        in_specs=[pl.BlockSpec(memory_space=pltpu.VMEM)] * 2,
        out_specs=pl.BlockSpec(memory_space=pltpu.VMEM),
        scratch_shapes=[pltpu.VMEM((2, 4, group, pulses // 2, n), jnp.float32)],
        compiler_params=pltpu.CompilerParams(vmem_limit_bytes=24 << 20),
        name="doppler",
    )(rows, samples)


def repack_kernel(echoes_ref, out_ref, sems):
    owners = out_ref.shape[0]
    step = owners // sems.shape[1]
    copies = [
        pltpu.make_async_copy(
            echoes_ref.at[part, pl.ds(k * step, step)],
            out_ref.at[pl.ds(k * step, step), part],
            sems.at[part, k],
        )
        for part in range(2)
        for k in range(sems.shape[1])
    ]
    for copy in copies:
        copy.start()
    for copy in copies:
        copy.wait()


def repack(echoes):
    shape = (echoes.shape[1], 2) + echoes.shape[2:]
    return pl.pallas_call(
        repack_kernel,
        out_shape=jax.ShapeDtypeStruct(shape, echoes.dtype),
        in_specs=[pl.BlockSpec(memory_space=pltpu.HBM)],
        out_specs=pl.BlockSpec(memory_space=pltpu.VMEM),
        scratch_shapes=[pltpu.SemaphoreType.DMA((2, 4))],
        compiler_params=pltpu.CompilerParams(vmem_limit_bytes=8 << 20),
        name="repack",
    )(echoes)


def covariance_kernel(total_gates, phase_ref, samples_ref, out_ref):
    sizes = dict(zip(EXCHANGE, samples_ref.shape))
    bins, _, gates, n = samples_ref.shape[5:]
    pa_count = sizes["xl"] * sizes["y"] * sizes["core"]
    row_count = sizes["z"] * sizes["xh"]
    taps = phase_ref.shape[1]
    reach = 2
    tile = taps // reach
    owners = tile // gates
    tiles_row = pa_count // owners
    scaling = 1.0 / math.sqrt(taps)

    def band(values):
        values = (values * scaling).astype(jnp.bfloat16).astype(jnp.float32)
        values = jnp.concatenate([values, jnp.zeros((1, tile), jnp.float32)], axis=1)
        values = jnp.broadcast_to(values, (tile, taps + tile))
        return pltpu.roll(values, 0, 1, stride=1, stride_axis=0).astype(jnp.bfloat16)

    real_band, imag_band = band(jnp.cos(phase_ref[...])), band(-jnp.sin(phase_ref[...]))
    parts = [slice(k * tile, (k + 1) * tile) for k in range(reach + 1)]
    bands = [jnp.concatenate([real_band[:, k], imag_band[:, k]], axis=1) for k in parts]
    bands = jnp.concatenate(bands, axis=0)
    carried = [None] * reach
    filtered = []
    ready = []
    tiles = row_count * tiles_row
    grams = [jnp.zeros((2 * n, 2 * n), jnp.float32)] * bins

    def added(rows):
        columns = [rows[:, b * 2 * n : (b + 1) * 2 * n] for b in range(bins)]
        return [
            gram
            + lax.dot_general(
                one, one, (((0,), (0,)), ((), ())), preferred_element_type=jnp.float32
            )
            for gram, one in zip(grams, columns)
        ]

    for t in reversed(range(tiles)):
        row, first = t // tiles_row, t % tiles_row * owners
        z, xh = divmod(row, sizes["xh"])
        xl, y = divmod(first // sizes["core"], sizes["y"])
        ys = slice(y, y + owners // sizes["core"])
        columns = []
        for b in range(bins):
            real, imag = (
                samples_ref[z, ys, xh, xl, :, b, part].reshape(tile, n) for part in range(2)
            )
            upper = jnp.concatenate([real, imag], axis=1)
            lower = jnp.concatenate([-imag, real], axis=1)
            columns.append(jnp.concatenate([upper, lower], axis=0))
        columns = jnp.concatenate(columns, axis=1)
        product = jnp.dot(bands, columns, preferred_element_type=jnp.float32)
        sums = [product[k] for k in parts]
        sums = [x if y is None else x + y for x, y in zip(sums, carried + [None])]
        carried = sums[1:]
        filtered.append(sums[0].astype(jnp.bfloat16))
        if len(filtered) == tiles // 2:
            if ready:
                grams = added(jnp.concatenate(ready, axis=0))
            ready, filtered = filtered, []
    grams = added(jnp.concatenate(ready, axis=0))
    for b, gram in enumerate(grams):
        out_ref[b, 0] = (gram[:n, :n] + gram[n:, n:]) / total_gates
        out_ref[b, 1] = (gram[n:, :n] - gram[:n, n:]) / total_gates


def covariances(phase, samples, total_gates):
    bins, element_count = samples.shape[5], samples.shape[-1]
    return pl.pallas_call(
        functools.partial(covariance_kernel, total_gates),
        out_shape=jax.ShapeDtypeStruct((bins, 2, element_count, element_count), jnp.float32),
        in_specs=[pl.BlockSpec(memory_space=pltpu.VMEM)] * 2,
        out_specs=pl.BlockSpec(memory_space=pltpu.VMEM),
        compiler_params=pltpu.CompilerParams(vmem_limit_bytes=24 << 20),
        name="covariances",
    )(phase, samples)


def per_device(echoes, chirp_phase):
    gates_dev, pulses_dev, element_count = echoes.shape[1:]
    sizes = {axis: lax.axis_size(axis) for axis in PA + ROW}
    pa_count, row_count = math.prod(sizes[a] for a in PA), math.prod(sizes[a] for a in ROW)
    pulses, total_gates = pulses_dev * pa_count, gates_dev * row_count
    devices = pa_count * row_count
    gates = gates_dev // pa_count
    bins = pulses // devices
    owners = np.arange(devices).reshape([sizes[a] for a in PA + ROW])
    order = owners.transpose([(PA + ROW).index(a) for a in EXCHANGE]).reshape(-1)
    position = np.argsort(order)
    places = [int(position[b // bins]) * bins + b % bins for b in range(pulses)]
    blocks = echoes.reshape(2, pa_count, gates, pulses_dev, element_count)
    blocks = repack(pltpu.with_memory_space_constraint(blocks, pltpu.HBM))
    turned = lax.all_to_all(blocks, PA, split_axis=0, concat_axis=0, tiled=True)
    spectrum = doppler(jnp.asarray(doppler_rows(pulses)), turned, places)
    spectrum = spectrum.reshape(devices, bins, 2, gates, element_count)
    owned = lax.all_to_all(spectrum, EXCHANGE, split_axis=0, concat_axis=0, tiled=True)
    owned = owned.reshape([sizes[a] for a in EXCHANGE] + [bins, 2, gates, element_count])
    return covariances(chirp_phase[None], owned, total_gates)


def solution(mesh):
    pa_count, row_count = mesh.shape["pa"], mesh.shape["row"]
    devices = mesh.devices.reshape(2, pa_count // 4, 2, row_count // 2, 2)
    return jax.shard_map(
        per_device,
        mesh=Mesh(devices, PA + ROW),
        in_specs=(P(None, ROW, PA, None), P()),
        out_specs=P(PA + ROW, None, None, None),
        check_vma=False,
    )
```

```python
import functools
import math

import jax
import jax.numpy as jnp
import numpy as np
from jax import lax
from jax.experimental import pallas as pl
from jax.experimental.pallas import tpu as pltpu
from jax.sharding import PartitionSpec as P


def doppler_rows(pulses):
    half = pulses // 2
    products = np.arange(half + 1)[:, None] * np.arange(pulses)[None, :] % pulses
    angles = (np.float32(2.0 * math.pi / pulses) * products.astype(np.float32)).astype(np.float64)
    scaling = 1.0 / math.sqrt(pulses)
    rows = np.concatenate([np.cos(angles), np.sin(angles[1:half])], axis=0) * scaling
    return rows.astype(np.float32).astype(jnp.bfloat16)


def doppler_kernel(rows_ref, samples_ref, out_ref, scratch):
    pulses = rows_ref.shape[0]
    half = pulses // 2
    gates, n = out_ref.shape[1:]
    slots, _, group = scratch.shape[:3]
    step = 8
    top = lax.broadcasted_iota(jnp.int32, (step, n), 0) == 0

    def turn(first, slot, low, high):
        for kind in range(4):
            for row in range(low, high, step):
                block = jnp.transpose(scratch[slot, kind, :, row : row + step, :], (1, 0, 2))
                block = block.astype(jnp.bfloat16)
                for j in range(step):
                    b = row + j
                    if kind >= 2:
                        b = pulses - b if b else half
                    out_ref[2 * b + kind % 2, first : first + group] = block[j]

    for first in range(0, gates, group):
        slot = first // group % slots
        for k in range(group):
            parts = [samples_ref[:, part, first + k].reshape(-1, n) for part in range(2)]
            product = jnp.dot(
                rows_ref[...], jnp.concatenate(parts, axis=1), preferred_element_type=jnp.float32
            )
            cos_real, cos_imag = product[:half, :n], product[:half, n:]
            sin_real, sin_imag = product[half:, :n], product[half:, n:]
            values = (
                cos_real + sin_imag,
                cos_imag - sin_real,
                cos_real - sin_imag,
                cos_imag + sin_real,
            )
            tops = (cos_real, cos_imag, sin_real, sin_imag)
            for kind in range(4):
                scratch[slot, kind, k] = values[kind]
                scratch[slot, kind, k, :step] = jnp.where(top, tops[kind][:step], values[kind][:step])
            if first:
                turn(first - group, 1 - slot, half * k // group, half * (k + 1) // group)
    turn(gates - group, (gates // group - 1) % slots, 0, half)


def doppler(rows, samples):
    gates, _, n = samples.shape[2:]
    pulses = rows.shape[0]
    group = math.gcd(16, gates)
    return pl.pallas_call(
        doppler_kernel,
        out_shape=jax.ShapeDtypeStruct((2 * pulses, gates, n), jnp.bfloat16),
        in_specs=[pl.BlockSpec(memory_space=pltpu.VMEM)] * 2,
        out_specs=pl.BlockSpec(memory_space=pltpu.VMEM),
        scratch_shapes=[pltpu.VMEM((2, 4, group, pulses // 2, n), jnp.float32)],
        compiler_params=pltpu.CompilerParams(vmem_limit_bytes=24 << 20),
        name="doppler",
    )(rows, samples)


REACH = 2


def band_rows(phase):
    taps = phase.shape[1]
    tile = taps // REACH
    scaling = 1.0 / math.sqrt(taps)

    def band(values):
        values = (values * scaling).astype(jnp.bfloat16).astype(jnp.float32)
        values = jnp.concatenate([values, jnp.zeros((1, tile), jnp.float32)], axis=1)
        values = jnp.broadcast_to(values, (tile, taps + tile))
        return pltpu.roll(values, 0, 1, stride=1, stride_axis=0).astype(jnp.bfloat16)

    real_band, imag_band = band(jnp.cos(phase)), band(-jnp.sin(phase))
    parts = [slice(k * tile, (k + 1) * tile) for k in range(REACH + 1)]
    bands = [jnp.concatenate([real_band[:, k], imag_band[:, k]], axis=1) for k in parts]
    return jnp.concatenate(bands, axis=0)


def repack_kernel(phase_ref, echoes_ref, out_ref, bands_ref, phase, phase_sem, sems):
    owners = out_ref.shape[0]
    step = owners // sems.shape[1]
    copies = [
        pltpu.make_async_copy(
            echoes_ref.at[part, pl.ds(k * step, step)],
            out_ref.at[pl.ds(k * step, step), part],
            sems.at[part, k],
        )
        for part in range(2)
        for k in range(sems.shape[1])
    ]
    fetch = pltpu.make_async_copy(phase_ref, phase, phase_sem)
    fetch.start()
    for copy in copies:
        copy.start()
    fetch.wait()
    bands_ref[...] = band_rows(phase[...])
    for copy in copies:
        copy.wait()


def repack(phase, echoes):
    shape = (echoes.shape[1], 2) + echoes.shape[2:]
    tile = phase.shape[1] // REACH
    return pl.pallas_call(
        repack_kernel,
        out_shape=[
            jax.ShapeDtypeStruct(shape, echoes.dtype),
            jax.ShapeDtypeStruct(((REACH + 1) * tile, 2 * tile), jnp.bfloat16),
        ],
        in_specs=[pl.BlockSpec(memory_space=pltpu.HBM)] * 2,
        out_specs=[pl.BlockSpec(memory_space=pltpu.VMEM)] * 2,
        scratch_shapes=[
            pltpu.VMEM(phase.shape, phase.dtype),
            pltpu.SemaphoreType.DMA,
            pltpu.SemaphoreType.DMA((2, 4)),
        ],
        compiler_params=pltpu.CompilerParams(vmem_limit_bytes=8 << 20),
        name="repack",
    )(phase, echoes)


def covariance_kernel(total_gates, bands_ref, samples_ref, out_ref):
    pa_count, row_count, bins, _, gates, n = samples_ref.shape
    bands = bands_ref[...]
    tile = bands.shape[1] // 2
    owners = tile // gates
    tiles_row = pa_count // owners
    parts = [slice(k * tile, (k + 1) * tile) for k in range(REACH + 1)]
    carried = [None] * REACH
    filtered = []
    for t in reversed(range(row_count * tiles_row)):
        row, first = t // tiles_row, t % tiles_row * owners
        columns = []
        for b in range(bins):
            real, imag = (
                samples_ref[first : first + owners, row, b, part].reshape(tile, n) for part in range(2)
            )
            upper = jnp.concatenate([real, imag], axis=1)
            lower = jnp.concatenate([-imag, real], axis=1)
            columns.append(jnp.concatenate([upper, lower], axis=0))
        columns = jnp.concatenate(columns, axis=1)
        product = jnp.dot(bands, columns, preferred_element_type=jnp.float32)
        sums = [product[k] for k in parts]
        sums = [x if y is None else x + y for x, y in zip(sums, carried + [None])]
        carried = sums[1:]
        filtered.append(sums[0].astype(jnp.bfloat16))
    filtered = jnp.concatenate(filtered, axis=0)
    for b in range(bins):
        one = filtered[:, b * 2 * n : (b + 1) * 2 * n]
        gram = lax.dot_general(
            one, one, (((0,), (0,)), ((), ())), preferred_element_type=jnp.float32
        )
        out_ref[b, 0] = (gram[:n, :n] + gram[n:, n:]) / total_gates
        out_ref[b, 1] = (gram[n:, :n] - gram[:n, n:]) / total_gates


def covariances(bands, samples, total_gates):
    bins, element_count = samples.shape[2], samples.shape[-1]
    return pl.pallas_call(
        functools.partial(covariance_kernel, total_gates),
        out_shape=jax.ShapeDtypeStruct((bins, 2, element_count, element_count), jnp.float32),
        in_specs=[pl.BlockSpec(memory_space=pltpu.VMEM)] * 2,
        out_specs=pl.BlockSpec(memory_space=pltpu.VMEM),
        compiler_params=pltpu.CompilerParams(vmem_limit_bytes=24 << 20),
        name="covariances",
    )(bands, samples)


def per_device(echoes, chirp_phase):
    gates_dev, pulses_dev, element_count = echoes.shape[1:]
    pa_count, row_count = lax.axis_size("pa"), lax.axis_size("row")
    pulses, total_gates = pulses_dev * pa_count, gates_dev * row_count
    devices = pa_count * row_count
    gates = gates_dev // pa_count
    bins = pulses // devices
    blocks = echoes.reshape(2, pa_count, gates, pulses_dev, element_count)
    blocks = pltpu.with_memory_space_constraint(blocks, pltpu.HBM)
    phase = pltpu.with_memory_space_constraint(chirp_phase[None], pltpu.HBM)
    blocks, bands = repack(phase, blocks)
    turned = lax.all_to_all(blocks, "pa", split_axis=0, concat_axis=0, tiled=True)
    spectrum = doppler(jnp.asarray(doppler_rows(pulses)), turned)
    spectrum = spectrum.reshape(devices, bins, 2, gates, element_count)
    owned = lax.all_to_all(spectrum, ("pa", "row"), split_axis=0, concat_axis=0, tiled=True)
    owned = owned.reshape(pa_count, row_count, bins, 2, gates, element_count)
    return covariances(bands, owned, total_gates)


def solution(mesh):
    placed = (P(None, "row", "pa", None), P())
    return jax.shard_map(
        per_device,
        mesh=mesh,
        in_specs=placed,
        out_specs=P(("pa", "row"), None, None, None),
        check_vma=False,
    )
```

```python
import functools
import math

import jax
import jax.numpy as jnp
import numpy as np
from jax import lax
from jax.experimental import pallas as pl
from jax.experimental.pallas import tpu as pltpu
from jax.sharding import PartitionSpec as P


def doppler_rows(pulses):
    half = pulses // 2
    products = np.arange(half + 1)[:, None] * np.arange(pulses)[None, :] % pulses
    angles = (np.float32(2.0 * math.pi / pulses) * products.astype(np.float32)).astype(np.float64)
    scaling = 1.0 / math.sqrt(pulses)
    rows = np.concatenate([np.cos(angles), np.sin(angles[1:half])], axis=0) * scaling
    return rows.astype(np.float32).astype(jnp.bfloat16)


def doppler_kernel(rows_ref, samples_ref, out_ref, scratch):
    pulses = rows_ref.shape[0]
    half = pulses // 2
    gates, n = out_ref.shape[1:]
    slots, _, group = scratch.shape[:3]
    step = 8
    top = lax.broadcasted_iota(jnp.int32, (step, n), 0) == 0

    def turn(first, slot, low, high):
        for kind in range(4):
            for row in range(low, high, step):
                block = jnp.transpose(scratch[slot, kind, :, row : row + step, :], (1, 0, 2))
                block = block.astype(jnp.bfloat16)
                for j in range(step):
                    b = row + j
                    if kind >= 2:
                        b = pulses - b if b else half
                    out_ref[2 * b + kind % 2, first : first + group] = block[j]

    for first in range(0, gates, group):
        slot = first // group % slots
        for k in range(group):
            parts = [samples_ref[:, part, first + k].reshape(-1, n) for part in range(2)]
            product = jnp.dot(
                rows_ref[...], jnp.concatenate(parts, axis=1), preferred_element_type=jnp.float32
            )
            cos_real, cos_imag = product[:half, :n], product[:half, n:]
            sin_real, sin_imag = product[half:, :n], product[half:, n:]
            values = (
                cos_real + sin_imag,
                cos_imag - sin_real,
                cos_real - sin_imag,
                cos_imag + sin_real,
            )
            tops = (cos_real, cos_imag, sin_real, sin_imag)
            for kind in range(4):
                scratch[slot, kind, k] = values[kind]
                scratch[slot, kind, k, :step] = jnp.where(top, tops[kind][:step], values[kind][:step])
            if first:
                turn(first - group, 1 - slot, half * k // group, half * (k + 1) // group)
    turn(gates - group, (gates // group - 1) % slots, 0, half)


def doppler(rows, samples):
    gates, _, n = samples.shape[2:]
    pulses = rows.shape[0]
    group = math.gcd(16, gates)
    return pl.pallas_call(
        doppler_kernel,
        out_shape=jax.ShapeDtypeStruct((2 * pulses, gates, n), jnp.bfloat16),
        in_specs=[pl.BlockSpec(memory_space=pltpu.VMEM)] * 2,
        out_specs=pl.BlockSpec(memory_space=pltpu.VMEM),
        scratch_shapes=[pltpu.VMEM((2, 4, group, pulses // 2, n), jnp.float32)],
        compiler_params=pltpu.CompilerParams(vmem_limit_bytes=24 << 20),
        name="doppler",
    )(rows, samples)


REACH = 2


def band_rows(phase):
    taps = phase.shape[1]
    tile = taps // REACH
    scaling = 1.0 / math.sqrt(taps)

    def band(values):
        values = (values * scaling).astype(jnp.bfloat16).astype(jnp.float32)
        values = jnp.concatenate([values, jnp.zeros((1, tile), jnp.float32)], axis=1)
        values = jnp.broadcast_to(values, (tile, taps + tile))
        return pltpu.roll(values, 0, 1, stride=1, stride_axis=0).astype(jnp.bfloat16)

    real_band, imag_band = band(jnp.cos(phase)), band(-jnp.sin(phase))
    parts = [slice(k * tile, (k + 1) * tile) for k in range(REACH + 1)]
    bands = [jnp.concatenate([real_band[:, k], imag_band[:, k]], axis=1) for k in parts]
    return jnp.concatenate(bands, axis=0)


def repack_kernel(phase_ref, echoes_ref, out_ref, bands_ref, phase, phase_sem, sems):
    owners = out_ref.shape[0]
    step = owners // sems.shape[1]
    copies = [
        pltpu.make_async_copy(
            echoes_ref.at[part, pl.ds(k * step, step)],
            out_ref.at[pl.ds(k * step, step), part],
            sems.at[part, k],
        )
        for part in range(2)
        for k in range(sems.shape[1])
    ]
    fetch = pltpu.make_async_copy(phase_ref, phase, phase_sem)
    fetch.start()
    for copy in copies:
        copy.start()
    fetch.wait()
    bands_ref[...] = band_rows(phase[...])
    for copy in copies:
        copy.wait()


def repack(phase, echoes):
    shape = (echoes.shape[1], 2) + echoes.shape[2:]
    tile = phase.shape[1] // REACH
    return pl.pallas_call(
        repack_kernel,
        out_shape=[
            jax.ShapeDtypeStruct(shape, echoes.dtype),
            jax.ShapeDtypeStruct(((REACH + 1) * tile, 2 * tile), jnp.bfloat16),
        ],
        in_specs=[pl.BlockSpec(memory_space=pltpu.HBM)] * 2,
        out_specs=[pl.BlockSpec(memory_space=pltpu.VMEM)] * 2,
        scratch_shapes=[
            pltpu.VMEM(phase.shape, phase.dtype),
            pltpu.SemaphoreType.DMA,
            pltpu.SemaphoreType.DMA((2, 4)),
        ],
        compiler_params=pltpu.CompilerParams(vmem_limit_bytes=8 << 20),
        name="repack",
    )(phase, echoes)


def covariance_kernel(total_gates, bands_ref, samples_ref, out_ref, result, sems):
    pa_count, row_count, bins, _, gates, n = samples_ref.shape
    bands = bands_ref[...]
    tile = bands.shape[1] // 2
    owners = tile // gates
    tiles_row = pa_count // owners
    parts = [slice(k * tile, (k + 1) * tile) for k in range(REACH + 1)]
    carried = [None] * REACH
    filtered = []
    for t in reversed(range(row_count * tiles_row)):
        row, first = t // tiles_row, t % tiles_row * owners
        columns = []
        for b in range(bins):
            real, imag = (
                samples_ref[first : first + owners, row, b, part].reshape(tile, n) for part in range(2)
            )
            upper = jnp.concatenate([real, imag], axis=1)
            lower = jnp.concatenate([-imag, real], axis=1)
            columns.append(jnp.concatenate([upper, lower], axis=0))
        columns = jnp.concatenate(columns, axis=1)
        product = jnp.dot(bands, columns, preferred_element_type=jnp.float32)
        sums = [product[k] for k in parts]
        sums = [x if y is None else x + y for x, y in zip(sums, carried + [None])]
        carried = sums[1:]
        filtered.append(sums[0].astype(jnp.bfloat16))
    filtered = jnp.concatenate(filtered, axis=0)
    for b in range(bins):
        one = filtered[:, b * 2 * n : (b + 1) * 2 * n]
        gram = lax.dot_general(
            one, one, (((0,), (0,)), ((), ())), preferred_element_type=jnp.float32
        )
        result[b, 0] = (gram[:n, :n] + gram[n:, n:]) / total_gates
        result[b, 1] = (gram[n:, :n] - gram[:n, n:]) / total_gates
        pltpu.make_async_copy(result.at[b], out_ref.at[b], sems.at[b]).start()
    for b in range(bins):
        pltpu.make_async_copy(result.at[b], out_ref.at[b], sems.at[b]).wait()


def covariances(bands, samples, total_gates):
    bins, element_count = samples.shape[2], samples.shape[-1]
    return pl.pallas_call(
        functools.partial(covariance_kernel, total_gates),
        out_shape=jax.ShapeDtypeStruct((bins, 2, element_count, element_count), jnp.float32),
        in_specs=[pl.BlockSpec(memory_space=pltpu.VMEM)] * 2,
        out_specs=pl.BlockSpec(memory_space=pltpu.HBM),
        scratch_shapes=[
            pltpu.VMEM((bins, 2, element_count, element_count), jnp.float32),
            pltpu.SemaphoreType.DMA((bins,)),
        ],
        compiler_params=pltpu.CompilerParams(vmem_limit_bytes=24 << 20),
        name="covariances",
    )(bands, samples)


def per_device(echoes, chirp_phase):
    gates_dev, pulses_dev, element_count = echoes.shape[1:]
    pa_count, row_count = lax.axis_size("pa"), lax.axis_size("row")
    pulses, total_gates = pulses_dev * pa_count, gates_dev * row_count
    devices = pa_count * row_count
    gates = gates_dev // pa_count
    bins = pulses // devices
    blocks = echoes.reshape(2, pa_count, gates, pulses_dev, element_count)
    blocks = pltpu.with_memory_space_constraint(blocks, pltpu.HBM)
    phase = pltpu.with_memory_space_constraint(chirp_phase[None], pltpu.HBM)
    blocks, bands = repack(phase, blocks)
    turned = lax.all_to_all(blocks, "pa", split_axis=0, concat_axis=0, tiled=True)
    spectrum = doppler(jnp.asarray(doppler_rows(pulses)), turned)
    spectrum = spectrum.reshape(devices, bins, 2, gates, element_count)
    owned = lax.all_to_all(spectrum, ("pa", "row"), split_axis=0, concat_axis=0, tiled=True)
    owned = owned.reshape(pa_count, row_count, bins, 2, gates, element_count)
    return covariances(bands, owned, total_gates)


def solution(mesh):
    placed = (P(None, "row", "pa", None), P())
    return jax.shard_map(
        per_device,
        mesh=mesh,
        in_specs=placed,
        out_specs=P(("pa", "row"), None, None, None),
        check_vma=False,
    )
```

```python
import functools
import math

import jax
import jax.numpy as jnp
import numpy as np
from jax import lax
from jax.experimental import pallas as pl
from jax.experimental.pallas import tpu as pltpu
from jax.sharding import PartitionSpec as P


def doppler_rows(pulses):
    half = pulses // 2
    products = np.arange(half + 1)[:, None] * np.arange(pulses)[None, :] % pulses
    angles = (np.float32(2.0 * math.pi / pulses) * products.astype(np.float32)).astype(np.float64)
    scaling = 1.0 / math.sqrt(pulses)
    rows = np.concatenate([np.cos(angles), np.sin(angles[1:half])], axis=0) * scaling
    return rows.astype(np.float32).astype(jnp.bfloat16)


def doppler_kernel(rows_ref, samples_ref, out_ref, scratch):
    pulses = rows_ref.shape[0]
    half = pulses // 2
    gates, n = out_ref.shape[1:]
    slots, _, group = scratch.shape[:3]
    step = 8
    top = lax.broadcasted_iota(jnp.int32, (step, n), 0) == 0

    def turn(first, slot, low, high):
        for kind in range(4):
            for row in range(low, high, step):
                block = jnp.transpose(scratch[slot, kind, :, row : row + step, :], (1, 0, 2))
                block = block.astype(jnp.bfloat16)
                for j in range(step):
                    b = row + j
                    if kind >= 2:
                        b = pulses - b if b else half
                    out_ref[2 * b + kind % 2, first : first + group] = block[j]

    for first in range(0, gates, group):
        slot = first // group % slots
        for k in range(group):
            parts = [samples_ref[:, part, first + k].reshape(-1, n) for part in range(2)]
            product = jnp.dot(
                rows_ref[...], jnp.concatenate(parts, axis=1), preferred_element_type=jnp.float32
            )
            cos_real, cos_imag = product[:half, :n], product[:half, n:]
            sin_real, sin_imag = product[half:, :n], product[half:, n:]
            values = (
                cos_real + sin_imag,
                cos_imag - sin_real,
                cos_real - sin_imag,
                cos_imag + sin_real,
            )
            tops = (cos_real, cos_imag, sin_real, sin_imag)
            for kind in range(4):
                scratch[slot, kind, k] = values[kind]
                scratch[slot, kind, k, :step] = jnp.where(top, tops[kind][:step], values[kind][:step])
            if first:
                turn(first - group, 1 - slot, half * k // group, half * (k + 1) // group)
    turn(gates - group, (gates // group - 1) % slots, 0, half)


def doppler(rows, samples):
    gates, _, n = samples.shape[2:]
    pulses = rows.shape[0]
    group = math.gcd(16, gates)
    return pl.pallas_call(
        doppler_kernel,
        out_shape=jax.ShapeDtypeStruct((2 * pulses, gates, n), jnp.bfloat16),
        in_specs=[pl.BlockSpec(memory_space=pltpu.VMEM)] * 2,
        out_specs=pl.BlockSpec(memory_space=pltpu.VMEM),
        scratch_shapes=[pltpu.VMEM((2, 4, group, pulses // 2, n), jnp.float32)],
        compiler_params=pltpu.CompilerParams(vmem_limit_bytes=24 << 20),
        name="doppler",
    )(rows, samples)


REACH = 2


def band_rows(phase):
    taps = phase.shape[1]
    tile = taps // REACH
    scaling = 1.0 / math.sqrt(taps)

    def band(values):
        values = (values * scaling).astype(jnp.bfloat16).astype(jnp.float32)
        values = jnp.concatenate([values, jnp.zeros((1, tile), jnp.float32)], axis=1)
        values = jnp.broadcast_to(values, (tile, taps + tile))
        return pltpu.roll(values, 0, 1, stride=1, stride_axis=0).astype(jnp.bfloat16)

    real_band, imag_band = band(jnp.cos(phase)), band(-jnp.sin(phase))
    parts = [slice(k * tile, (k + 1) * tile) for k in range(REACH + 1)]
    bands = [jnp.concatenate([real_band[:, k], imag_band[:, k]], axis=1) for k in parts]
    return jnp.concatenate(bands, axis=0)


def repack_kernel(phase_ref, echoes_ref, out_ref, bands_ref, phase, phase_sem, sems):
    owners = out_ref.shape[0]
    step = owners // sems.shape[1]
    copies = [
        pltpu.make_async_copy(
            echoes_ref.at[part, pl.ds(k * step, step)],
            out_ref.at[pl.ds(k * step, step), part],
            sems.at[part, k],
        )
        for part in range(2)
        for k in range(sems.shape[1])
    ]
    fetch = pltpu.make_async_copy(phase_ref, phase, phase_sem)
    fetch.start()
    for copy in copies:
        copy.start()
    fetch.wait()
    bands_ref[...] = band_rows(phase[...])
    for copy in copies:
        copy.wait()


def repack(phase, echoes):
    shape = (echoes.shape[1], 2) + echoes.shape[2:]
    tile = phase.shape[1] // REACH
    return pl.pallas_call(
        repack_kernel,
        out_shape=[
            jax.ShapeDtypeStruct(shape, echoes.dtype),
            jax.ShapeDtypeStruct(((REACH + 1) * tile, 2 * tile), jnp.bfloat16),
        ],
        in_specs=[pl.BlockSpec(memory_space=pltpu.HBM)] * 2,
        out_specs=[pl.BlockSpec(memory_space=pltpu.VMEM)] * 2,
        scratch_shapes=[
            pltpu.VMEM(phase.shape, phase.dtype),
            pltpu.SemaphoreType.DMA,
            pltpu.SemaphoreType.DMA((2, 4)),
        ],
        compiler_params=pltpu.CompilerParams(vmem_limit_bytes=8 << 20),
        name="repack",
    )(phase, echoes)


def covariance_kernel(total_gates, bands_ref, samples_ref, out_ref):
    pa_count, row_count, bins, _, gates, n = samples_ref.shape
    bands = bands_ref[...]
    tile = bands.shape[1] // 2
    owners = tile // gates
    tiles_row = pa_count // owners
    parts = [slice(k * tile, (k + 1) * tile) for k in range(REACH + 1)]
    carried = [None] * REACH
    filtered = []
    for t in reversed(range(row_count * tiles_row)):
        row, first = t // tiles_row, t % tiles_row * owners
        columns = []
        for b in range(bins):
            real, imag = (
                samples_ref[first : first + owners, row, b, part].reshape(tile, n) for part in range(2)
            )
            upper = jnp.concatenate([real, imag], axis=1)
            lower = jnp.concatenate([-imag, real], axis=1)
            columns.append(jnp.concatenate([upper, lower], axis=0))
        columns = jnp.concatenate(columns, axis=1)
        product = jnp.dot(bands, columns, preferred_element_type=jnp.float32)
        sums = [product[k] for k in parts]
        sums = [x if y is None else x + y for x, y in zip(sums, carried + [None])]
        carried = sums[1:]
        filtered.append(sums[0].astype(jnp.bfloat16))
    middle = len(filtered) // 2
    halves = [jnp.concatenate(h, axis=0) for h in (filtered[:middle], filtered[middle:])]
    for b in range(bins):
        ones = [half[:, b * 2 * n : (b + 1) * 2 * n] for half in halves]
        grams = [
            lax.dot_general(one, one, (((0,), (0,)), ((), ())), preferred_element_type=jnp.float32)
            for one in ones
        ]
        gram = grams[0] + grams[1]
        out_ref[b, 0] = (gram[:n, :n] + gram[n:, n:]) / total_gates
        out_ref[b, 1] = (gram[n:, :n] - gram[:n, n:]) / total_gates


def covariances(bands, samples, total_gates):
    bins, element_count = samples.shape[2], samples.shape[-1]
    return pl.pallas_call(
        functools.partial(covariance_kernel, total_gates),
        out_shape=jax.ShapeDtypeStruct((bins, 2, element_count, element_count), jnp.float32),
        in_specs=[pl.BlockSpec(memory_space=pltpu.VMEM)] * 2,
        out_specs=pl.BlockSpec(memory_space=pltpu.VMEM),
        compiler_params=pltpu.CompilerParams(vmem_limit_bytes=24 << 20),
        name="covariances",
    )(bands, samples)


def per_device(echoes, chirp_phase):
    gates_dev, pulses_dev, element_count = echoes.shape[1:]
    pa_count, row_count = lax.axis_size("pa"), lax.axis_size("row")
    pulses, total_gates = pulses_dev * pa_count, gates_dev * row_count
    devices = pa_count * row_count
    gates = gates_dev // pa_count
    bins = pulses // devices
    blocks = echoes.reshape(2, pa_count, gates, pulses_dev, element_count)
    blocks = pltpu.with_memory_space_constraint(blocks, pltpu.HBM)
    phase = pltpu.with_memory_space_constraint(chirp_phase[None], pltpu.HBM)
    blocks, bands = repack(phase, blocks)
    turned = lax.all_to_all(blocks, "pa", split_axis=0, concat_axis=0, tiled=True)
    spectrum = doppler(jnp.asarray(doppler_rows(pulses)), turned)
    spectrum = spectrum.reshape(devices, bins, 2, gates, element_count)
    owned = lax.all_to_all(spectrum, ("pa", "row"), split_axis=0, concat_axis=0, tiled=True)
    owned = owned.reshape(pa_count, row_count, bins, 2, gates, element_count)
    return covariances(bands, owned, total_gates)


def solution(mesh):
    placed = (P(None, "row", "pa", None), P())
    return jax.shard_map(
        per_device,
        mesh=mesh,
        in_specs=placed,
        out_specs=P(("pa", "row"), None, None, None),
        check_vma=False,
    )
```
